32 devices in a mesh: seq: 32 (over z, y, x, core).
Axes of the slice: x: 2, y: 2, z: 4, core: 2. Of those that a mesh axis runs over, the one named last changes fastest.
Arguments:
- tokens: bfloat16 [12288, 768], P('seq'), may hold values from -6 to 6
- cotangent: bfloat16 [12288, 768], P('seq'), may hold values from -6 to 6
- offsets: int32 [9], replicated, may hold values from 0 to 12287, as said below
- gain_in: bfloat16 [2, 768], P(None, 'seq'), may hold values from 0.099609375 to 1.8984375
- w_in: bfloat16 [2, 768, 3376], P(None, 'seq'), may hold values from -0.21875 to 0.21875
- conv_w: bfloat16 [2, 1792, 7], P(None, 'seq'), may hold values from -2 to 2
- conv_b: bfloat16 [2, 1792], P(None, 'seq'), may hold values from -3 to 3
- gain_out: bfloat16 [2, 1536], P(None, 'seq'), may hold values from 0.099609375 to 1.8984375
- w_out: bfloat16 [2, 1536, 768], P(None, 'seq'), may hold values from -0.15625 to 0.15625
- head_params: float32 [2, 4, 24], replicated, may hold values from -13 to 1.5
Outputs:
- result: bfloat16 [12288, 768], P('seq')
- grad_tokens: float32 [12288, 768], P('seq')
- grad_gain_in: float32 [2, 768], P(None, 'seq')
- grad_w_in: float32 [2, 768, 3376], P(None, 'seq')
- grad_conv_w: float32 [2, 1792, 7], P(None, 'seq')
- grad_conv_b: float32 [2, 1792], P(None, 'seq')
- grad_gain_out: float32 [2, 1536], P(None, 'seq')
- grad_w_out: float32 [2, 1536, 768], P(None, 'seq')
- grad_head_params: float32 [2, 4, 24], replicated
The draws below stay inside these ranges and needn't reach their ends.
Inputs may be any that keep to these rules, and one draw needn't show every extreme that they name: offsets[0] = 0 and they rise strictly; offsets[8] = 12287, so the last token is padding; one sequence starts within the first 192 tokens and ends after token 12096.
All inputs are finite; a program needn't handle non-finite values.
Results may differ from the reference program's by a relative error of at most 0.025.
Values may be sent and summed in bfloat16 or wider, within the bound.
No kernel may reach another device: no remote copies, remote signals or barrier semaphores. Data moves between devices by JAX's collectives and lax.ppermute only.
A program may use at most 832 MiB of HBM per device.

```python
import jax
import jax.numpy as jnp
from jax import lax

D = 768
HEADS = 24
HEAD = 64
STATE = 64
CONV = 4
SPAN = 128
LAYERS = 2
NSEQ = 8
TOK_DEV = 384
INNER = 1536
CONVW = 1792
PROJ = 3376
TOKENS = 12288


def draw_offsets(key, part):
    subkeys = jax.random.split(key, 2)
    small_lengths = jax.random.randint(subkeys[0], (NSEQ,), 1, TOK_DEV // 16 + 1)
    chosen = jax.random.randint(subkeys[1], (), 0, NSEQ)
    padding = 1
    picked = jnp.arange(NSEQ) == chosen
    others = jnp.sum(jnp.where(picked, 0, small_lengths))
    lengths = jnp.where(picked, TOKENS - padding - others, small_lengths)
    return jnp.concatenate([jnp.zeros((1,), jnp.int32), jnp.cumsum(lengths)]).astype(jnp.int32)


def draw_head_params(key, part):
    subkeys = jax.random.split(key, 5)
    ranking = jax.vmap(lambda single: jax.random.permutation(single, HEADS))(jax.random.split(subkeys[0], LAYERS * 2)).reshape(LAYERS, 2, HEADS)
    slow_count = HEADS // 2
    rate_log = jax.random.uniform(subkeys[1], (LAYERS, 1, HEADS), jnp.float32, -0.7, 0.7)
    slow_bias = jax.random.uniform(subkeys[2], (LAYERS, 2, HEADS), jnp.float32, -13.0, -12.0)
    fast_bias = jax.random.uniform(subkeys[3], (LAYERS, 2, HEADS), jnp.float32, -4.2, -3.2)
    biases = jnp.where(ranking < slow_count, slow_bias, fast_bias)
    skips = jax.random.uniform(subkeys[4], (LAYERS, 1, HEADS), jnp.float32, 0.5, 1.5)
    return jnp.concatenate([rate_log, biases, skips], axis=1).astype(jnp.float32)


def block_levels(key, shape, cuts, least, high):
    level, own = 1.0, jax.random.fold_in(key, 6)
    for dim, shards_of in cuts:
        heights = jnp.exp(jax.random.uniform(jax.random.fold_in(own, dim), (shards_of,), jnp.float32, least / len(cuts), high / len(cuts)))
        level = level * jnp.repeat(heights, shape[dim] // shards_of).reshape([-1 if axis == dim else 1 for axis in range(len(shape))])
    return level


def noise(rng, shape, deviation, bound, cuts=(), kind=jnp.bfloat16):
    drawn = deviation * jax.random.normal(rng, shape, jnp.float32)
    if cuts:
        drawn = drawn * block_levels(rng, shape, cuts, -0.22, 0.18)
    return jnp.clip(drawn, -bound, bound).astype(kind)


def setup_inputs(seed: int = 0) -> dict:
    key_list = jax.random.split(jax.random.key(seed), 11)
    tokens = noise(key_list[0], (TOKENS, D), 1.0, 6.0, ((0, 32),))
    cotangent = noise(key_list[1], (TOKENS, D), 1.0, 6.0, ((0, 32),))
    offsets = draw_offsets(jax.random.fold_in(key_list[10], 71), 0)
    gain_in = jnp.clip(1.0 + 0.18 * jax.random.normal(key_list[3], (LAYERS, D), jnp.float32), 0.099609375, 1.8984375).astype(jnp.bfloat16)
    w_in = noise(key_list[4], (LAYERS, D, PROJ), D ** -0.5, 0.21875, ((1, 32),))
    conv_w = noise(key_list[5], (LAYERS, CONVW, 2 * CONV - 1), (2 * CONV - 1) ** -0.5, 2.0, ((1, 32),))
    conv_b = noise(key_list[6], (LAYERS, CONVW), 0.5, 3.0, ((1, 32),))
    gain_out = jnp.clip(1.0 + 0.18 * jax.random.normal(key_list[7], (LAYERS, INNER), jnp.float32), 0.099609375, 1.8984375).astype(jnp.bfloat16)
    w_out = noise(key_list[8], (LAYERS, INNER, D), INNER ** -0.5, 0.15625, ((1, 32),))
    head_params = draw_head_params(jax.random.fold_in(key_list[10], 71), 0)
    return dict(tokens=tokens, cotangent=cotangent, offsets=offsets, gain_in=gain_in, w_in=w_in, conv_w=conv_w, conv_b=conv_b, gain_out=gain_out, w_out=w_out, head_params=head_params)


@jax.custom_vjp
def low(v):
    return lax.optimization_barrier(v.astype(jnp.bfloat16)).astype(jnp.float32)

@jax.custom_vjp
def low_back(v):
    return v

def low_keep(v):
    return (low(v), None)

def low_pass(kept, grad):
    return (grad,)

def back_keep(v):
    return (v, None)

def back_low(kept, grad):
    return (low(grad),)
low.defvjp(low_keep, low_pass)
low_back.defvjp(back_keep, back_low)
precise = lax.Precision.HIGHEST
epsilon = 1e-05

def segment_of(offsets, positions, extent):
    counted = lax.optimization_barrier(jnp.sum((offsets[None, :] <= positions[:, None]).astype(jnp.int32), axis=1)) - 1
    inside = jnp.where(positions < 0, -1, counted)
    return jnp.where(positions >= extent, -2, inside).astype(jnp.int32)

def block_step(carried, block_data):
    state_now, previous = carried
    values, writes, reads, steps, decays, labels = block_data
    extent = labels.shape[0]
    cumulative = jnp.cumsum(decays, axis=0)
    scores = jnp.dot(reads, writes.T, precision=precise)
    places = jnp.arange(extent)
    linked = (labels[:, None] == labels[None, :]) & (places[:, None] > places[None, :])
    log_gap = jnp.minimum(cumulative[:, None, :] - cumulative[None, :, :], 0.0)
    mixing = jnp.where(linked[:, :, None], jnp.exp(log_gap), 0.0) * scores[:, :, None]
    inputs = values * steps[:, :, None]
    within = jnp.einsum('tsh,shp->thp', mixing, inputs, precision=precise)
    entering = jnp.where((labels == previous)[:, None], jnp.exp(cumulative), 0.0)
    from_state = jnp.einsum('tn,hpn->thp', reads, state_now, precision=precise) * entering[:, :, None]
    final_label = labels[extent - 1]
    trailing = jnp.where((labels == final_label)[:, None], jnp.exp(cumulative[extent - 1][None, :] - cumulative), 0.0)
    through = jnp.where(final_label == previous, jnp.exp(cumulative[extent - 1]), 0.0)
    added_state = jnp.einsum('sh,shp,sn->hpn', trailing, inputs, writes, precision=precise)
    return ((state_now * through[:, None, None] + added_state, final_label), within + from_state)

def scan_direction(step_function, values, writes, reads, steps, decays, labels, previous, state_in):
    number = labels.shape[0] // SPAN

    def blocked(tensor):
        return tensor.reshape((number, SPAN) + tensor.shape[1:])
    final_carry, outputs = lax.scan(step_function, (state_in, previous), (blocked(values), blocked(writes), blocked(reads), blocked(steps), blocked(decays), blocked(labels)))
    return (outputs.reshape(values.shape), final_carry[0])

def conv_mix(bordered, conv_w, conv_b, labels, labels_rim):
    extent = labels.shape[0]
    pre_act = jnp.zeros((extent, conv_b.shape[0]), jnp.float32) + conv_b[None, :]
    for tap_index in range(2 * CONV - 1):
        linked = (labels_rim[tap_index:tap_index + extent] == labels).astype(jnp.float32)
        pre_act = pre_act + conv_w[:, tap_index][None, :] * bordered[tap_index:tap_index + extent] * linked[:, None]
    return pre_act

def mixer_layer(hidden, gain_in, w_in, conv_w, conv_b, gain_out, w_out, head_table, labels, labels_rim, present):
    extent = hidden.shape[0]
    factor = lax.rsqrt(lax.optimization_barrier(jnp.mean(hidden * hidden, axis=1, keepdims=True)) + epsilon)
    normed_in = low(hidden * factor * gain_in[None, :])
    projected = low_back(jnp.dot(normed_in, w_in, precision=precise))
    gate_values = projected[:, :INNER]
    channels = low(projected[:, INNER:INNER + CONVW])
    raw_steps = projected[:, INNER + CONVW:]
    bordered = jnp.pad(channels, ((CONV - 1, CONV - 1), (0, 0)))
    pre_act = low_back(conv_mix(bordered, conv_w, conv_b, labels, labels_rim))
    activated = low(jax.nn.silu(pre_act) * present[:, None])
    values = activated[:, :INNER].reshape(extent, HEADS, HEAD)
    write_fore = activated[:, INNER:INNER + STATE]
    read_fore = activated[:, INNER + STATE:INNER + 2 * STATE]
    write_back = activated[:, INNER + 2 * STATE:INNER + 3 * STATE]
    read_back = activated[:, INNER + 3 * STATE:]
    decay_rate = jnp.exp(head_table[0])
    step_fore = jax.nn.softplus(raw_steps[:, :HEADS] + head_table[1][None, :])
    step_back = jax.nn.softplus(raw_steps[:, HEADS:] + head_table[2][None, :])
    zero_state = jnp.zeros((HEADS, HEAD, STATE), jnp.float32)
    stepper = jax.checkpoint(block_step)
    mixed_fore, unused = scan_direction(stepper, values, write_fore, read_fore, step_fore, -decay_rate[None, :] * step_fore, labels, jnp.array(-1, jnp.int32), zero_state)
    mixed_back, unused = scan_direction(stepper, values[::-1], write_back[::-1], read_back[::-1], step_back[::-1], (-decay_rate[None, :] * step_back)[::-1], labels[::-1], jnp.array(-2, jnp.int32), zero_state)
    merged = mixed_fore + mixed_back[::-1] + head_table[3][None, :, None] * values
    gated_heads = merged * jax.nn.silu(gate_values).reshape(extent, HEADS, HEAD)
    head_scale = lax.rsqrt(lax.optimization_barrier(jnp.mean(gated_heads * gated_heads, axis=2, keepdims=True)) + epsilon)
    normed_out = low((gated_heads * head_scale).reshape(extent, INNER) * gain_out[None, :])
    return hidden + low_back(jnp.dot(normed_out, w_out, precision=precise))

def reference(tokens, cotangent, offsets, gain_in, w_in, conv_w, conv_b, gain_out, w_out, head_params):
    extent = tokens.shape[0]
    positions = jnp.arange(extent, dtype=jnp.int32)
    labels = segment_of(offsets, positions, extent)
    labels_rim = segment_of(offsets, jnp.arange(-(CONV - 1), extent + CONV - 1, dtype=jnp.int32), extent)
    present = (positions < offsets[NSEQ]).astype(jnp.float32)

    def forward(hidden, gains_in, weights_in, conv_taps, biases, gains_out, weights_out, head_all):
        for layer_index in range(LAYERS):
            hidden = mixer_layer(hidden, gains_in[layer_index], weights_in[layer_index], conv_taps[layer_index], biases[layer_index], gains_out[layer_index], weights_out[layer_index], head_all[layer_index], labels, labels_rim, present)
        return hidden
    primals = (tokens.astype(jnp.float32), gain_in.astype(jnp.float32), w_in.astype(jnp.float32), conv_w.astype(jnp.float32), conv_b.astype(jnp.float32), gain_out.astype(jnp.float32), w_out.astype(jnp.float32), head_params)
    result, pullback = jax.vjp(forward, *primals)
    gradients = pullback(cotangent.astype(jnp.float32))
    return (result.astype(jnp.bfloat16), gradients[0], gradients[1], gradients[2], gradients[3], gradients[4], gradients[5], gradients[6], gradients[7])
```

```python
import functools

import jax
import jax.numpy as jnp
from jax import lax
from jax.experimental import pallas as pl
from jax.experimental.pallas import tpu as pltpu
from jax.sharding import PartitionSpec as P

HEADS = 24
HEAD = 64
STATE = 64
CONV = 4
SPAN = 128
LAYERS = 2
NSEQ = 8
INNER = 1536
CONVW = 1792
ROWS = 1920
TILE = 256
LANES = 128
RIM = 8
epsilon = 1e-05
bf16 = jnp.bfloat16
f32 = jnp.float32
AXIS = "seq"
PLANE = 4
VMEM_LIMIT = 56 * 1024 * 1024

NN = (((1,), (0,)), ((), ()))
NT = (((1,), (1,)), ((), ()))
TN = (((0,), (0,)), ((), ()))


def dot(a, b, dims=NN):
    return lax.dot_general(a, b, dims, preferred_element_type=f32)


def dot_exact(a, b, dims=NN):
    return lax.dot_general(
        a, b, dims, precision=lax.Precision.HIGHEST, preferred_element_type=f32
    )


def sigmoid(v):
    return 1.0 / (1.0 + jnp.exp(-v))


def softplus(v):
    return jnp.maximum(v, 0.0) + jnp.log1p(jnp.exp(-jnp.abs(v)))


def segment(pos, scalars):
    count = jnp.zeros(pos.shape, jnp.int32) - 1
    for j in range(NSEQ + 1):
        count = count + jnp.where(scalars[2 + j] <= pos, 1, 0)
    count = jnp.where(pos < 0, -1, count)
    return jnp.where(pos >= scalars[1], -2, count)


def iota(shape, axis):
    return lax.broadcasted_iota(jnp.int32, shape, axis)


def spread(coef, onehot):
    high = coef.astype(bf16)
    low = (coef - high.astype(f32)).astype(bf16)
    return dot(jnp.concatenate([high, low], axis=1), onehot)


def gather_heads(values, onehot):
    return dot(values.astype(bf16), onehot[:LANES], NT)


def chunk_marks(scalars, c):
    start = scalars[0] + c * SPAN
    col = segment(start + iota((SPAN, LANES), 0), scalars)
    row = segment(start + iota((1, SPAN), 1), scalars)
    spot = jnp.zeros((1, LANES), jnp.int32) + start
    return (
        col,
        row,
        segment(spot - 1, scalars),
        segment(spot, scalars),
        segment(spot + SPAN - 1, scalars),
        segment(spot + SPAN, scalars),
    )


def edge_weights(kum, total, marks):
    col, _, before, first, last, after = marks
    ahead = iota((SPAN, LANES), 1) < HEADS
    ahead_row = iota((1, LANES), 1) < HEADS
    from_start = jnp.exp(kum)
    to_end = jnp.exp(total - kum)
    near = jnp.where(ahead_row, before, after)
    far = jnp.where(ahead_row, last, first)
    enter = jnp.where(col == near, jnp.where(ahead, from_start, to_end), 0.0)
    leave = jnp.where(col == far, jnp.where(ahead, to_end, from_start), 0.0)
    passing = jnp.where(far == near, jnp.exp(total), 0.0)
    return enter, leave, passing


def chunk_total(kum_ref, la_row, c):
    last = kum_ref[pl.ds(c * SPAN + SPAN - 8, 8), :][7:8, :]
    ahead = iota((1, LANES), 1) < HEADS
    return jnp.where(ahead, last, last + la_row)


def rows8(parts):
    top = jnp.concatenate(parts, axis=0)
    return jnp.concatenate([top, jnp.zeros((8 - top.shape[0], top.shape[1]), top.dtype)], axis=0)


def state_slices(scalars, which, other, bundle, keep_ref, send_ref):
    half = STATE // 2
    for index, ref in ((which, keep_ref), (other, send_ref)):
        for part, state in enumerate(bundle[:2]):
            ref[pl.ds(part * half, half), :] = state[pl.ds(pl.multiple_of(index * half, half), half), :].astype(ref.dtype)
        ref[pl.ds(2 * half, 8), :] = bundle[2].astype(ref.dtype)


def enter_kernel(
    scalars,
    h_ref,
    low_ref,
    high_ref,
    gain_ref,
    w_ref,
    taps_ref,
    head_ref,
    hotf_ref,
    hotr_ref,
    xn_ref,
    rows_ref,
    act_ref,
    dsl_ref,
    dt_ref,
    kum_ref,
    sig_ref,
    tot_ref,
    loc_ref,
    keep_ref,
    send_ref,
    ext_ref,
    lab_ref,
    shift_ref,
    la_ref,
    dev_ref,
):
    extent = h_ref.shape[0]
    wide = extent + 2 * RIM

    def normed(h):
        scale = lax.rsqrt(jnp.mean(h * h, axis=1, keepdims=True) + epsilon)
        return (h * scale * gain_ref[...]).astype(bf16)

    own = normed(h_ref[...])
    xn_ref[...] = own
    ext_ref[pl.ds(0, RIM), :] = normed(low_ref[...])
    ext_ref[pl.ds(RIM, extent), :] = own
    ext_ref[pl.ds(RIM + extent, RIM), :] = normed(high_ref[...])
    lab_ref[...] = segment(scalars[0] - RIM + iota((wide, LANES), 0), scalars)
    lab = lab_ref[pl.ds(RIM, extent), :]
    valid = jnp.where(scalars[0] + iota((extent, LANES), 0) < scalars[2 + NSEQ], 1.0, 0.0)
    valid2 = jnp.concatenate([valid, valid], axis=1)
    masks = []
    for k in range(2 * CONV - 1):
        same = jnp.where(lab_ref[pl.ds(RIM + k - CONV + 1, extent), :] == lab, 1.0, 0.0)
        masks.append(jnp.concatenate([same, same], axis=1))

    def tile(j, carry):
        at = pl.ds(pl.multiple_of(j * TILE, TILE), TILE)
        rows = dot(ext_ref[...], w_ref[:, at]).astype(bf16)
        rows_ref[:, at] = rows
        shift_ref[...] = rows.astype(f32)
        taps = taps_ref[:, at]
        pre = jnp.zeros((extent, TILE), f32) + taps[7:8]
        for k in range(2 * CONV - 1):
            moved = shift_ref[pl.ds(RIM + k - CONV + 1, extent), :]
            pre = pre + taps[k : k + 1] * (moved if k == CONV - 1 else moved * masks[k])
        sig = sigmoid(pre)
        act_ref[:, at] = (pre * sig * valid2).astype(bf16)
        dsl_ref[:, at] = (sig * (1.0 + pre * (1.0 - sig)) * valid2).astype(bf16)
        return carry

    lax.fori_loop(0, CONVW // TILE, tile, 0)
    raw = dot(xn_ref[...], w_ref[:, CONVW:])
    shifted = raw + head_ref[1:2]
    dt = softplus(shifted)
    dt_ref[...] = dt
    sig_ref[...] = sigmoid(shifted)
    la_ref[...] = dt * head_ref[0:1]
    tri = jnp.where(iota((SPAN, SPAN), 0) >= iota((SPAN, SPAN), 1), 1.0, 0.0)
    ahead = iota((SPAN, LANES), 1) < HEADS
    chunks = extent // SPAN
    for c in range(chunks):
        at = pl.ds(c * SPAN, SPAN)
        la = la_ref[at, :]
        full = dot_exact(tri, la)
        total = full[SPAN - 1 :]
        kum = jnp.where(ahead, full, full - la)
        kum_ref[at, :] = kum
        enter, leave, passing = edge_weights(kum, total, chunk_marks(scalars, c))
        coef = leave * dt_ref[at, :]
        tot_ref[pl.ds(c * 8, 8), :] = rows8([total, passing])
        x = act_ref[at, :INNER].astype(f32)
        for d, hot in enumerate((hotf_ref, hotr_ref)):
            scaled = (x * spread(coef, hot[...])).astype(bf16)
            b = act_ref[at, pl.ds(INNER + 2 * STATE * d, STATE)]
            loc_ref[d, c] = dot(b, scaled, TN)
    devices = []
    for d, hot in enumerate((hotf_ref, hotr_ref)):
        state = None
        whole = None
        for c in range(chunks) if d == 0 else reversed(range(chunks)):
            passing = spread(tot_ref[pl.ds(c * 8, 8), :], hot[...])[1:2]
            state = loc_ref[d, c] if state is None else loc_ref[d, c] + passing * state
            whole = passing if whole is None else whole * passing
        dev_ref[d] = state
        devices.append(whole)
    state_slices(
        scalars, scalars[11], 1 - scalars[11], (dev_ref.at[0], dev_ref.at[1], rows8(devices)), keep_ref, send_ref
    )


def within_kernel(scalars, act_ref, dt_ref, kum_ref, skip_ref, y_ref):
    chunks = act_ref.shape[0] // SPAN

    def chunk(c, carry):
        at = pl.ds(pl.multiple_of(c * SPAN, SPAN), SPAN)
        col, row = chunk_marks(scalars, c)[:2]
        t, s = iota((SPAN, SPAN), 0), iota((SPAN, SPAN), 1)
        low = t > s
        bc = act_ref[at, INNER:]
        fore = dot(bc[:, STATE : 2 * STATE], bc[:, :STATE], NT)
        back = dot(bc[:, 3 * STATE :], bc[:, 2 * STATE : 3 * STATE], NT)
        scores = jnp.where(low, fore, back)
        scores = jnp.where((col == row) & (t != s), scores, 0.0)
        kum = kum_ref[at, :]
        kum_t = kum.T
        dt_t = dt_ref[at, :].T
        left = iota((SPAN, LANES), 1) < HEAD
        for pair in range(HEADS // 2):
            mixes = []
            for h in (2 * pair, 2 * pair + 1):
                r = HEADS + h
                gap = jnp.where(
                    low, kum[:, h : h + 1] - kum_t[h : h + 1], kum_t[r : r + 1] - kum[:, r : r + 1]
                )
                step = jnp.where(low, dt_t[h : h + 1], dt_t[r : r + 1])
                mixes.append((jnp.exp(jnp.minimum(gap, 0.0)) * scores * step).astype(bf16))
            lanes = pl.ds(pair * LANES, LANES)
            x = act_ref[at, lanes]
            none = jnp.zeros_like(x)
            stacked = jnp.concatenate([jnp.where(left, x, none), jnp.where(left, none, x)], axis=0)
            y_ref[at, lanes] = dot(jnp.concatenate(mixes, axis=1), stacked) + skip_ref[:, pair * LANES : pair * LANES + LANES] * x.astype(f32)
        return carry

    lax.fori_loop(0, chunks, chunk, 0)


def joined_states(scalars, own_ref, got_ref, d):
    half = STATE // 2
    own = own_ref[pl.ds(d * half, half), :].astype(f32)
    got = got_ref[pl.ds(d * half, half), :].astype(f32)
    first = scalars[11] == 0
    return jnp.concatenate([jnp.where(first, own, got), jnp.where(first, got, own)], axis=0)


def leave_kernel(
    scalars,
    y_in_ref,
    gate_ref,
    act_ref,
    kum_ref,
    tot_ref,
    loc_ref,
    own_ref,
    got_ref,
    gain_ref,
    w_ref,
    h_ref,
    hotf_ref,
    hotr_ref,
    h_out_ref,
    y_ref,
    sin_ref,
):
    extent = h_ref.shape[0]
    chunks = extent // SPAN
    hots = (hotf_ref, hotr_ref)
    for d in range(2):
        state = joined_states(scalars, own_ref, got_ref, d)
        for c in range(chunks) if d == 0 else reversed(range(chunks)):
            sin_ref[d, c] = state.astype(bf16)
            passing = spread(tot_ref[pl.ds(c * 8, 8), :], hots[d][...])[1:2]
            state = loc_ref[d, c] + passing * state
    for c in range(chunks):
        at = pl.ds(c * SPAN, SPAN)
        enter, _, _ = edge_weights(kum_ref[at, :], tot_ref[c * 8 : c * 8 + 1, :], chunk_marks(scalars, c))
        y = y_in_ref[at, :]
        for d in range(2):
            reads = act_ref[at, pl.ds(INNER + 2 * STATE * d, 2 * STATE)][:, STATE:]
            y = y + dot(reads, sin_ref[d, c]) * spread(enter, hots[d][...])
        y_ref[at, :] = y
        gate = gate_ref[at, :]
        m = y * (gate * sigmoid(gate))
        scale = lax.rsqrt(gather_heads(m * m, hotf_ref[...]) * (1.0 / HEAD) + epsilon)
        out = (m * spread(scale, hotf_ref[...]) * gain_ref[...]).astype(bf16)
        h_out_ref[at, :] = h_ref[at, :] + dot(out, w_ref[...])


def gate_kernel(
    scalars,
    g_ref,
    w_ref,
    y_ref,
    gate_ref,
    gain_ref,
    act_ref,
    kum_ref,
    tot_ref,
    hotf_ref,
    hotr_ref,
    gb_ref,
    yn_ref,
    dy_ref,
    dgate_ref,
    sums_ref,
    loc_ref,
    keep_ref,
    send_ref,
    dev_ref,
):
    extent = g_ref.shape[0]
    chunks = extent // SPAN
    hots = (hotf_ref, hotr_ref)
    gain_sum = jnp.zeros((1, INNER), f32)
    skip_sum = jnp.zeros((1, INNER), f32)
    for c in range(chunks):
        at = pl.ds(c * SPAN, SPAN)
        gb = g_ref[at, :].astype(bf16)
        gb_ref[at, :] = gb
        dyn = dot(gb, w_ref[...], NT)
        y = y_ref[at, :]
        gate = gate_ref[at, :]
        sig = sigmoid(gate)
        silu = gate * sig
        m = y * silu
        scale_h = lax.rsqrt(gather_heads(m * m, hotf_ref[...]) * (1.0 / HEAD) + epsilon)
        scale = spread(scale_h, hotf_ref[...])
        normed = m * scale
        yn_ref[at, :] = (normed * gain_ref[...]).astype(bf16)
        gain_sum = gain_sum + jnp.sum(dyn * normed, axis=0, keepdims=True)
        q = dyn * gain_ref[...]
        mean = gather_heads(q * m, hotf_ref[...]) * (1.0 / HEAD)
        dm = scale * q - m * spread(mean * scale_h * scale_h * scale_h, hotf_ref[...])
        dy = dm * silu
        dyb = dy.astype(bf16)
        dy_ref[at, :] = dyb
        dgate_ref[at, :] = (dm * y * sig * (1.0 + gate * (1.0 - sig))).astype(bf16)
        skip_sum = skip_sum + jnp.sum(dy * act_ref[at, :INNER].astype(f32), axis=0, keepdims=True)
        enter, _, _ = edge_weights(kum_ref[at, :], tot_ref[c * 8 : c * 8 + 1, :], chunk_marks(scalars, c))
        for d in range(2):
            reads = act_ref[at, pl.ds(INNER + 2 * STATE * d, 2 * STATE)][:, STATE:]
            loc_ref[d, c] = dot(reads, (dy * spread(enter, hots[d][...])).astype(bf16), TN)
    sums_ref[...] = rows8([gain_sum, skip_sum])
    devices = []
    for d in range(2):
        state = None
        whole = None
        for c in range(chunks) if d == 1 else reversed(range(chunks)):
            passing = spread(tot_ref[pl.ds(c * 8, 8), :], hots[d][...])[1:2]
            state = loc_ref[d, c] if state is None else loc_ref[d, c] + passing * state
            whole = passing if whole is None else whole * passing
        dev_ref[d] = state
        devices.append(whole)
    state_slices(
        scalars,
        scalars[11],
        1 - scalars[11],
        (dev_ref.at[1], dev_ref.at[0], rows8([devices[1], devices[0]])),
        keep_ref,
        send_ref,
    )


def within_back_kernel(scalars, act_ref, dt_ref, kum_ref, dy_ref, skip_ref, dx_ref, dbc_ref, ddt_ref, dk_ref):
    chunks = act_ref.shape[0] // SPAN

    def chunk(c, carry):
        at = pl.ds(pl.multiple_of(c * SPAN, SPAN), SPAN)
        col, row = chunk_marks(scalars, c)[:2]
        s, t = iota((SPAN, SPAN), 0), iota((SPAN, SPAN), 1)
        low = t > s
        bc = act_ref[at, INNER:]
        b_f, c_f = bc[:, :STATE], bc[:, STATE : 2 * STATE]
        b_r, c_r = bc[:, 2 * STATE : 3 * STATE], bc[:, 3 * STATE :]
        joined = (col == row) & (t != s)
        scores = jnp.where(joined, jnp.where(low, dot(b_f, c_f, NT), dot(b_r, c_r, NT)), 0.0)
        kum = kum_ref[at, :]
        kum_t = kum.T
        dt = dt_ref[at, :]
        lane = iota((SPAN, LANES), 1)
        sub = iota((LANES, SPAN), 0)
        left = lane < HEAD
        dscore = jnp.zeros((SPAN, SPAN), f32)
        ddt = jnp.zeros((SPAN, LANES), f32)
        dk_t = jnp.zeros((LANES, SPAN), f32)
        for pair in range(HEADS // 2):
            lanes = pl.ds(pair * LANES, LANES)
            x = act_ref[at, lanes]
            dy = dy_ref[at, lanes]
            none = jnp.zeros_like(x)
            dmix = dot(
                jnp.concatenate([jnp.where(left, x, none), jnp.where(left, none, x)], axis=0), dy, NT
            )
            mixes = []
            for i in range(2):
                h = 2 * pair + i
                r = HEADS + h
                gap = jnp.where(
                    low, kum_t[h : h + 1] - kum[:, h : h + 1], kum[:, r : r + 1] - kum_t[r : r + 1]
                )
                step = jnp.where(low, dt[:, h : h + 1], dt[:, r : r + 1])
                decay = jnp.exp(jnp.minimum(gap, 0.0))
                weight = decay * scores
                mixes.append((weight * step).astype(bf16))
                dw = dmix[i * SPAN : (i + 1) * SPAN]
                dscore = dscore + dw * (decay * step)
                p = dw * weight
                p_low = jnp.where(low, p, 0.0)
                p_up = p - p_low
                ddt_f = jnp.sum(p_low, axis=1, keepdims=True)
                ddt_r = jnp.sum(p_up, axis=1, keepdims=True)
                ddt = jnp.where(lane == h, ddt_f, jnp.where(lane == r, ddt_r, ddt))
                rsum_f = jnp.sum(p_low * step, axis=0, keepdims=True)
                rsum_r = jnp.sum(p_up * step, axis=0, keepdims=True)
                dk_t = jnp.where(sub == h, rsum_f, jnp.where(sub == r, -rsum_r, dk_t))
            stacked = jnp.concatenate([jnp.where(left, dy, none), jnp.where(left, none, dy)], axis=0)
            dx_ref[at, lanes] = dot(jnp.concatenate(mixes, axis=1), stacked) + skip_ref[:, pair * LANES : pair * LANES + LANES] * dy.astype(f32)
        ddt_ref[at, :] = ddt
        dk_ref[at, :] = dk_t.T + jnp.where(lane < HEADS, -1.0, 1.0) * ddt * dt
        d_low = jnp.where(joined & low, dscore, 0.0).astype(bf16)
        d_up = jnp.where(joined & jnp.logical_not(low), dscore, 0.0).astype(bf16)
        dbc_ref[at, :] = jnp.concatenate(
            [dot(d_low, c_f), dot(d_low, b_f, TN), dot(d_up, c_r), dot(d_up, b_r, TN)], axis=1
        )
        return carry

    lax.fori_loop(0, chunks, chunk, 0)


def across_back_kernel(
    scalars,
    act_ref,
    dt_ref,
    kum_ref,
    sig_ref,
    tot_ref,
    dy_ref,
    dx_ref,
    dbc_ref,
    ddt_ref,
    dk_ref,
    loc_ref,
    sin_ref,
    own_ref,
    got_ref,
    dsl_ref,
    head_ref,
    hotf_ref,
    hotr_ref,
    dpre_ref,
    draw_ref,
    sums_ref,
    sout_ref,
):
    extent = act_ref.shape[0]
    chunks = extent // SPAN
    hots = (hotf_ref, hotr_ref)
    for d in range(2):
        state = joined_states(scalars, own_ref, got_ref, 1 - d)
        for c in range(chunks) if d == 1 else reversed(range(chunks)):
            sout_ref[d, c] = state
            passing = spread(tot_ref[pl.ds(c * 8, 8), :], hots[d][...])[1:2]
            state = loc_ref[d, c] + passing * state
    ahead = iota((SPAN, LANES), 1) < HEADS
    a, b = iota((SPAN, SPAN), 0), iota((SPAN, SPAN), 1)
    rate_sum = jnp.zeros((1, LANES), f32)
    raw_sum = jnp.zeros((1, LANES), f32)
    for c in range(chunks):
        at = pl.ds(c * SPAN, SPAN)
        kum = kum_ref[at, :]
        dt = dt_ref[at, :]
        enter, leave, passing = edge_weights(kum, tot_ref[c * 8 : c * 8 + 1, :], chunk_marks(scalars, c))
        x = act_ref[at, :INNER].astype(f32)
        dy = dy_ref[at, :].astype(f32)
        dx = dx_ref[at, :]
        dbc = []
        ins, outs, thr = [], [], []
        for d in range(2):
            hot = hots[d][...]
            writes = act_ref[at, pl.ds(INNER + 2 * STATE * d, STATE)]
            reads = act_ref[at, pl.ds(INNER + 2 * STATE * d, 2 * STATE)][:, STATE:]
            s_in = sin_ref[d, c]
            s_out = sout_ref[d, c]
            s_out_b = s_out.astype(bf16)
            leave_w = spread(leave * dt, hot)
            dc = dot((dy * spread(enter, hot)).astype(bf16), s_in, NT)
            db = dot((x * leave_w).astype(bf16), s_out_b, NT)
            seen = dot(reads, s_in)
            given = dot(writes, s_out_b)
            dx = dx + given * leave_w
            ins.append(gather_heads(dy * seen, hot))
            outs.append(gather_heads(x * given, hot))
            thr.append(gather_heads(rows8([jnp.sum(s_in.astype(f32) * s_out, axis=0, keepdims=True)]), hot)[0:1])
            dbc += [db, dc]
        d_in = (ins[0] + ins[1]) * enter
        d_out = (outs[0] + outs[1]) * leave
        through = (thr[0] + thr[1]) * passing
        dt_out = d_out * dt
        dk = dk_ref[at, :]
        later = jnp.where(ahead, dk + d_in, 0.0)
        earlier = jnp.where(ahead, dt_out, 0.0)
        dla_f = dot_exact(jnp.where(b >= a, 1.0, 0.0), later) + dot_exact(jnp.where(b < a, 1.0, 0.0), earlier)
        upto = jnp.where(ahead, 0.0, d_in)
        beyond = jnp.where(ahead, 0.0, dt_out + dk)
        dla_r = dot_exact(jnp.where(b <= a, 1.0, 0.0), upto) + dot_exact(jnp.where(b > a, 1.0, 0.0), beyond)
        dla = dla_f + dla_r + through
        neg_rate = head_ref[0:1]
        ddt = ddt_ref[at, :] + d_out + neg_rate * dla
        draw = ddt * sig_ref[at, :]
        rate_sum = rate_sum + jnp.sum(dla * (dt * neg_rate), axis=0, keepdims=True)
        raw_sum = raw_sum + jnp.sum(draw, axis=0, keepdims=True)
        draw_ref[at, :] = jnp.where(iota((SPAN, LANES), 1) < 2 * HEADS, draw, 0.0).astype(bf16)
        dpre_ref[at, :INNER] = (dx * dsl_ref[at, :INNER].astype(f32)).astype(bf16)
        dbc = dbc_ref[at, :] + jnp.concatenate(dbc, axis=1)
        dpre_ref[at, INNER:] = (dbc * dsl_ref[at, INNER:].astype(f32)).astype(bf16)
    sums_ref[...] = rows8([rate_sum, raw_sum])


def taps_kernel(scalars, rows_ref, dpre_ref, dtaps_ref, shift_ref, lab_ref):
    extent = dpre_ref.shape[0]
    wide = extent + 2 * RIM
    lab_ref[...] = segment(scalars[0] - RIM + iota((wide, LANES), 0), scalars)
    lab = lab_ref[pl.ds(RIM, extent), :]
    masks = []
    for k in range(2 * CONV - 1):
        same = jnp.where(lab_ref[pl.ds(RIM + k - CONV + 1, extent), :] == lab, 1.0, 0.0)
        masks.append(jnp.concatenate([same, same], axis=1))

    def tile(j, carry):
        at = pl.ds(pl.multiple_of(j * TILE, TILE), TILE)
        dpre = dpre_ref[:, at].astype(f32)
        shift_ref[...] = rows_ref[:, at].astype(f32)
        parts = []
        for k in range(2 * CONV - 1):
            moved = shift_ref[pl.ds(RIM + k - CONV + 1, extent), :]
            parts.append(jnp.sum(dpre * (moved if k == CONV - 1 else moved * masks[k]), axis=0, keepdims=True))
        parts.append(jnp.sum(dpre, axis=0, keepdims=True))
        dtaps_ref[:, at] = jnp.concatenate(parts, axis=0)
        return carry

    lax.fori_loop(0, CONVW // TILE, tile, 0)


def proj_back_kernel(
    scalars, dpre_ref, low_ref, high_ref, taps_ref, draw_ref, xn_ref, dproj_ref, gw_ref, shift_ref, lab_ref
):
    extent = dpre_ref.shape[0]
    wide = extent + 2 * RIM
    lab_ref[...] = segment(scalars[0] - RIM + iota((wide, LANES), 0), scalars)
    lab = lab_ref[pl.ds(RIM, extent), :]
    masks = []
    for k in range(2 * CONV - 1):
        same = jnp.where(lab_ref[pl.ds(RIM + CONV - 1 - k, extent), :] == lab, 1.0, 0.0)
        masks.append(jnp.concatenate([same, same], axis=1))

    def tile(j, carry):
        at = pl.ds(pl.multiple_of(j * TILE, TILE), TILE)
        shift_ref[pl.ds(0, RIM), :] = low_ref[:, at].astype(f32)
        shift_ref[pl.ds(RIM, extent), :] = dpre_ref[:, at].astype(f32)
        shift_ref[pl.ds(RIM + extent, RIM), :] = high_ref[:, at].astype(f32)
        taps = taps_ref[:, at]
        drows = jnp.zeros((extent, TILE), f32)
        for k in range(2 * CONV - 1):
            moved = shift_ref[pl.ds(RIM + CONV - 1 - k, extent), :]
            drows = drows + taps[k : k + 1] * (moved if k == CONV - 1 else moved * masks[k])
        drows = drows.astype(bf16)
        dproj_ref[:, at] = drows
        gw_ref[:, at] = dot(xn_ref[...], drows, TN).astype(bf16)
        return carry

    lax.fori_loop(0, CONVW // TILE, tile, 0)
    draw = draw_ref[...]
    dproj_ref[:, CONVW:] = draw
    gw_ref[:, CONVW:] = dot(xn_ref[...], draw, TN).astype(bf16)


def norm_back_kernel(dproj_ref, dgate_ref, wr_ref, wg_ref, h_ref, gain_ref, g_ref, g_out_ref, sums_ref):
    dxn = dot(dproj_ref[...], wr_ref[...], NT) + dot(dgate_ref[...], wg_ref[...], NT)
    h = h_ref[...]
    factor = lax.rsqrt(jnp.mean(h * h, axis=1, keepdims=True) + epsilon)
    hr = h * factor
    sums_ref[...] = rows8([jnp.sum(dxn * hr, axis=0, keepdims=True)])
    q = dxn * gain_ref[...]
    g_out_ref[...] = (
        g_ref[...] + factor * q - hr * (factor * factor) * jnp.mean(q * h, axis=1, keepdims=True)
    )


def chip_kernel(scalars, keep_ref, got_ref, send_ref, own_ref):
    half = STATE // 2
    part = half // PLANE
    first = scalars[11] == 0
    keep = keep_ref[...].astype(f32)
    got = got_ref[...].astype(f32)
    early = jnp.where(first, keep, got)
    late = jnp.where(first, got, keep)
    d_early, d_late = early[2 * half : 2 * half + 8], late[2 * half : 2 * half + 8]
    fore = late[:half] + d_late[0:1] * early[:half]
    back = early[half : 2 * half] + d_early[1:2] * late[half : 2 * half]
    both = (d_early * d_late).astype(bf16)
    for j in range(PLANE):
        rows = slice(j * part, (j + 1) * part)
        send_ref[j, 0:part] = fore[rows].astype(bf16)
        send_ref[j, part : 2 * part] = back[rows].astype(bf16)
        send_ref[j, 2 * part :] = both
    own_ref[0:half] = early[:half]
    own_ref[half : 2 * half] = late[half : 2 * half]
    own_ref[2 * half :] = rows8([d_early[0:1], d_late[1:2]])


def plane_kernel(scalars, mine_ref, a_ref, b_ref, c_ref, send_ref, pre_ref, order_ref):
    part = STATE // 2 // PLANE
    chip = scalars[12]
    for m, ref in enumerate((mine_ref, a_ref, b_ref, c_ref)):
        order_ref[chip ^ m] = ref[...].astype(f32)
    fore = jnp.zeros((part, INNER), f32)
    back = jnp.zeros((part, INNER), f32)
    d_fore = jnp.ones((1, INNER), f32)
    d_back = jnp.ones((1, INNER), f32)
    for k in range(PLANE):
        j = k
        pre_ref[0, j] = fore
        pre_ref[2, j] = jnp.broadcast_to(d_fore, (part, INNER))
        dec = order_ref[j, 2 * part :][0:1]
        fore = order_ref[j, 0:part] + dec * fore
        d_fore = d_fore * dec
        j = PLANE - 1 - k
        pre_ref[1, j] = back
        pre_ref[3, j] = jnp.broadcast_to(d_back, (part, INNER))
        dec = order_ref[j, 2 * part :][1:2]
        back = order_ref[j, part : 2 * part] + dec * back
        d_back = d_back * dec
    decays = rows8([d_fore, d_back])
    send_ref[0] = jnp.concatenate([fore, decays], axis=0).astype(bf16)
    send_ref[1] = jnp.concatenate([back, decays], axis=0).astype(bf16)


def column_kernel(groups, scalars, pre_ref, *refs):
    got = refs[: groups - 1]
    out_ref, order_ref = refs[groups - 1 :]
    part = STATE // 2 // PLANE
    z = scalars[13]
    order_ref[z] = jnp.zeros((part + 8, INNER), f32)
    for m in range(1, groups):
        order_ref[z ^ m] = got[m - 1][...].astype(f32)
    fore = jnp.zeros((part, INNER), f32)
    back = jnp.zeros((part, INNER), f32)
    for k in range(groups):
        fore = jnp.where(k < z, order_ref[k, 0:part] + order_ref[k, part:][0:1] * fore, fore)
        j = groups - 1 - k
        back = jnp.where(j > z, order_ref[j, 0:part] + order_ref[j, part:][1:2] * back, back)
    for j in range(PLANE):
        out_ref[j, 0:part] = (pre_ref[0, j] + pre_ref[2, j] * fore).astype(bf16)
        out_ref[j, part:] = (pre_ref[1, j] + pre_ref[3, j] * back).astype(bf16)


def back_kernel(scalars, own_ref, mine_ref, a_ref, b_ref, c_ref, keep_ref, send_ref, order_ref):
    half = STATE // 2
    part = half // PLANE
    chip = scalars[12]
    for m, ref in enumerate((mine_ref, a_ref, b_ref, c_ref)):
        order_ref[chip ^ m] = ref[...].astype(f32)
    fore = jnp.concatenate([order_ref[j, 0:part] for j in range(PLANE)], axis=0)
    back = jnp.concatenate([order_ref[j, part:] for j in range(PLANE)], axis=0)
    decays = own_ref[2 * half :]
    fore_late = own_ref[0:half] + decays[0:1] * fore
    back_early = own_ref[half : 2 * half] + decays[1:2] * back
    early = jnp.concatenate([fore, back_early], axis=0).astype(bf16)
    late = jnp.concatenate([fore_late, back], axis=0).astype(bf16)
    first = scalars[11] == 0
    keep_ref[...] = jnp.where(first, early, late)
    send_ref[...] = jnp.where(first, late, early)


def whole(shape, dtype):
    return jax.ShapeDtypeStruct(shape, dtype)


def call(kernel, scalars, arrays, outs, scratch=(), flops=0, name=None):
    moved = sum(a.size * a.dtype.itemsize for a in arrays)
    moved += sum(o.size * o.dtype.itemsize for o in outs)
    smem = [pl.BlockSpec(memory_space=pltpu.SMEM)] if scalars is not None else []
    args = ([scalars] if scalars is not None else []) + list(arrays)
    return pl.pallas_call(
        kernel,
        out_shape=tuple(outs),
        in_specs=smem + [pl.BlockSpec(memory_space=pltpu.VMEM)] * len(arrays),
        out_specs=tuple(pl.BlockSpec(memory_space=pltpu.VMEM) for _ in outs),
        scratch_shapes=list(scratch),
        compiler_params=pltpu.CompilerParams(vmem_limit_bytes=VMEM_LIMIT),
        cost_estimate=pl.CostEstimate(flops=flops, bytes_accessed=moved, transcendentals=0),
        name=name,
    )(*args)


def partner(value, mask):
    count = lax.axis_size(AXIS)
    return lax.ppermute(value, AXIS, [(i, i ^ mask) for i in range(count)])


def exchange(scalars, keep, send):
    count = lax.axis_size(AXIS)
    groups = count // (2 * PLANE)
    place = lax.axis_index(AXIS)
    chip, z = (place // 2) % PLANE, place // (2 * PLANE)
    half, part = STATE // 2, STATE // 2 // PLANE
    got = partner(send, 1)
    cut, own = call(
        chip_kernel,
        scalars,
        (keep, got),
        (whole((PLANE, 2 * part + 8, INNER), bf16), whole((2 * half + 8, INNER), f32)),
        name="chip_states",
    )

    def to(chips, m):
        return lax.dynamic_index_in_dim(chips, chip ^ m, 0, False)

    around = [partner(to(cut, m), 2 * m) for m in range(1, PLANE)]
    total, pre = call(
        plane_kernel,
        scalars,
        (to(cut, 0), *around),
        (whole((2, part + 8, INNER), bf16), whole((4, PLANE, part, INNER), f32)),
        [pltpu.VMEM((PLANE, 2 * part + 8, INNER), f32)],
        name="plane_states",
    )
    column = []
    for m in range(1, groups):
        up = (z ^ m) > z
        column.append(partner(jnp.where(up, total[0], total[1]), 2 * PLANE * m))
    (entering,) = call(
        functools.partial(column_kernel, groups),
        scalars,
        (pre, *column),
        (whole((PLANE, 2 * part, INNER), bf16),),
        [pltpu.VMEM((groups, part + 8, INNER), f32)],
        name="column_states",
    )
    around = [partner(to(entering, m), 2 * m) for m in range(1, PLANE)]
    mine, theirs = call(
        back_kernel,
        scalars,
        (own, to(entering, 0), *around),
        (whole((2 * half, INNER), bf16), whole((2 * half, INNER), bf16)),
        [pltpu.VMEM((PLANE, 2 * part, INNER), f32)],
        name="core_states",
    )
    return mine, partner(theirs, 1)


def shares(count):
    groups = count // (2 * PLANE)
    return [core + 2 * p + 2 * PLANE * g for core in range(2) for p in range(PLANE) for g in range(groups)]


def by_owner(place, count):
    groups = count // (2 * PLANE)
    mask = jnp.arange(count, dtype=jnp.int32) ^ place
    position = (mask % 2) * (PLANE * groups) + ((mask // 2) % PLANE) * groups + mask // (2 * PLANE)
    return position, jnp.array(shares(count), jnp.int32) ^ place


def gathered(block):
    count = lax.axis_size(AXIS)
    groups = count // (2 * PLANE)
    part = jnp.stack([block] + [partner(block, 2 * PLANE * m) for m in range(1, groups)])
    part = jnp.concatenate([part] + [partner(part, 2 * m) for m in range(1, PLANE)], axis=0)
    return jnp.concatenate([part, partner(part, 1)], axis=0)


def summed(blocks):
    count = lax.axis_size(AXIS)
    groups = count // (2 * PLANE)
    half = count // 2
    dtype = blocks.dtype
    kept = (blocks[:half].astype(f32) + partner(blocks[half:], 1).astype(f32)).astype(dtype)
    total = kept[:groups].astype(f32)
    for m in range(1, PLANE):
        total = total + partner(kept[m * groups : (m + 1) * groups], 2 * m).astype(f32)
    kept = total.astype(dtype)
    total = kept[0].astype(f32)
    for m in range(1, groups):
        total = total + partner(kept[m], 2 * PLANE * m).astype(f32)
    return total


def everywhere(value):
    count = lax.axis_size(AXIS)
    groups = count // (2 * PLANE)
    value = value + partner(value, 1)
    value = value + sum(partner(value, 2 * m) for m in range(1, PLANE))
    return value + sum(partner(value, 2 * PLANE * m) for m in range(1, groups))


def ordered(stack, position):
    taken = jnp.take(stack, position, axis=0)
    return taken.reshape((taken.shape[0] * taken.shape[1],) + taken.shape[2:])


def rims(block):
    count = lax.axis_size(AXIS)
    length = block.shape[0]
    up = [(i, i + 1) for i in range(count - 1)]
    down = [(i + 1, i) for i in range(count - 1)]
    low = lax.ppermute(block[length - RIM :], AXIS, up)
    high = lax.ppermute(block[:RIM], AXIS, down)
    return low, high


def layer_forward(hidden, weights, scalars, hots):
    extent = hidden.shape[0]
    chunks = extent // SPAN
    low, high = rims(hidden)
    (xn, rows, act, dsl, dt, kum, sig, tot, loc, keep, send) = call(
        enter_kernel,
        scalars,
        (hidden, low, high, weights["gain_in"], weights["w_rows"], weights["taps"], weights["head"], *hots),
        (
            whole((extent, hidden.shape[1]), bf16),
            whole((extent + 2 * RIM, CONVW), bf16),
            whole((extent, CONVW), bf16),
            whole((extent, CONVW), bf16),
            whole((extent, LANES), f32),
            whole((extent, LANES), f32),
            whole((extent, LANES), f32),
            whole((chunks * 8, LANES), f32),
            whole((2, chunks, STATE, INNER), f32),
            whole((STATE + 8, INNER), bf16),
            whole((STATE + 8, INNER), bf16),
        ),
        [
            pltpu.VMEM((extent + 2 * RIM, hidden.shape[1]), bf16),
            pltpu.VMEM((extent + 2 * RIM, LANES), jnp.int32),
            pltpu.VMEM((extent + 2 * RIM, TILE), f32),
            pltpu.VMEM((extent, LANES), f32),
            pltpu.VMEM((2, STATE, INNER), f32),
        ],
        flops=2 * extent * hidden.shape[1] * ROWS,
        name="enter",
    )
    (y_in,) = call(
        within_kernel,
        scalars,
        (act, dt, kum, weights["skip"]),
        (whole((extent, INNER), f32),),
        flops=2 * extent * SPAN * INNER,
        name="within",
    )
    gate = dot(xn, weights["w_gate"])
    own, got = exchange(scalars, keep, send)
    out, y, sin = call(
        leave_kernel,
        scalars,
        (
            y_in,
            gate,
            act,
            kum,
            tot,
            loc,
            own,
            got,
            weights["gain_out"],
            weights["w_out"],
            hidden,
            *hots,
        ),
        (
            whole(hidden.shape, f32),
            whole((extent, INNER), f32),
            whole((2, chunks, STATE, INNER), bf16),
        ),
        flops=2 * extent * hidden.shape[1] * INNER,
        name="leave",
    )
    return out, (hidden, xn, rows, act, dsl, dt, kum, sig, tot, gate, y, sin)


def layer_backward(grad, stored, weights, scalars, hots, order):
    hidden, xn, rows, act, dsl, dt, kum, sig, tot, gate, y, sin = stored
    extent, width = hidden.shape
    chunks = extent // SPAN
    gb, yn, dy, dgate, sums_y, loc, keep, send = call(
        gate_kernel,
        scalars,
        (grad, weights["w_out"], y, gate, weights["gain_out"], act, kum, tot, *hots),
        (
            whole((extent, width), bf16),
            whole((extent, INNER), bf16),
            whole((extent, INNER), bf16),
            whole((extent, INNER), bf16),
            whole((8, INNER), f32),
            whole((2, chunks, STATE, INNER), f32),
            whole((STATE + 8, INNER), bf16),
            whole((STATE + 8, INNER), bf16),
        ),
        [pltpu.VMEM((2, STATE, INNER), f32)],
        flops=2 * extent * width * INNER,
        name="gate_back",
    )
    dx, dbc, ddt, dk = call(
        within_back_kernel,
        scalars,
        (act, dt, kum, dy, weights["skip"]),
        (
            whole((extent, INNER), f32),
            whole((extent, 4 * STATE), f32),
            whole((extent, LANES), f32),
            whole((extent, LANES), f32),
        ),
        flops=4 * extent * SPAN * INNER,
        name="within_back",
    )
    gw_out = dot(yn, gb, TN).astype(bf16)
    gw_gate = dot(xn, dgate, TN).astype(bf16)
    own, got = exchange(scalars, keep, send)
    dpre, draw, sums_h = call(
        across_back_kernel,
        scalars,
        (act, dt, kum, sig, tot, dy, dx, dbc, ddt, dk, loc, sin, own, got, dsl, weights["head"], *hots),
        (whole((extent, CONVW), bf16), whole((extent, LANES), bf16), whole((8, LANES), f32)),
        [pltpu.VMEM((2, chunks, STATE, INNER), f32)],
        flops=8 * extent * STATE * INNER,
        name="across_back",
    )
    low, high = rims(dpre)
    (dtaps,) = call(
        taps_kernel,
        scalars,
        (rows, dpre),
        (whole((8, CONVW), f32),),
        [pltpu.VMEM((extent + 2 * RIM, TILE), f32), pltpu.VMEM((extent + 2 * RIM, LANES), jnp.int32)],
        name="taps_back",
    )
    dproj, gw_rows = call(
        proj_back_kernel,
        scalars,
        (dpre, low, high, weights["taps"], draw, xn),
        (whole((extent, ROWS), bf16), whole((width, ROWS), bf16)),
        [pltpu.VMEM((extent + 2 * RIM, TILE), f32), pltpu.VMEM((extent + 2 * RIM, LANES), jnp.int32)],
        flops=2 * extent * width * ROWS,
        name="proj_back",
    )
    grad_in, sums_d = call(
        norm_back_kernel,
        None,
        (dproj, dgate, weights["w_rows"], weights["w_gate"], hidden, weights["gain_in"], grad),
        (whole((extent, width), f32), whole((8, width), f32)),
        flops=2 * extent * width * (ROWS + INNER),
        name="norm_back",
    )
    return grad_in, (gw_rows, gw_gate, gw_out, dtaps, sums_y, sums_h, sums_d)


def shard_program(tokens, cotangent, offsets, gain_in, w_in, conv_w, conv_b, gain_out, w_out, head_params):
    length, width = tokens.shape
    count = lax.axis_size(AXIS)
    place = lax.axis_index(AXIS)
    scalars = jnp.concatenate(
        [
            jnp.stack([place * length, jnp.int32(count * length)]),
            offsets,
            jnp.stack([place % 2, (place // 2) % PLANE, place // (2 * PLANE)]),
        ]
    ).astype(jnp.int32)
    position, owner = by_owner(place, count)
    k_index = jnp.arange(2 * LANES)[:, None] % LANES
    head_of = jnp.arange(INNER)[None, :] // HEAD
    hots = ((k_index == head_of).astype(bf16), (k_index == head_of + HEADS).astype(bf16))

    cw, gi, go = conv_w.shape[1], gain_in.shape[1], gain_out.shape[1]
    taps_count = 2 * CONV - 1
    small = jnp.concatenate(
        [conv_w.transpose(0, 2, 1).reshape(-1), conv_b.reshape(-1), gain_in.reshape(-1), gain_out.reshape(-1)]
    )
    small_len = small.shape[0]
    small_rows = -(-small_len // (8 * LANES)) * 8
    small = jnp.pad(small, (0, small_rows * LANES - small_len)).reshape(small_rows, LANES)
    small = jnp.take(gathered(small).reshape(count, small_rows * LANES), position, axis=0).astype(f32)
    at = 0

    def taken(*shape):
        nonlocal at
        size = 1
        for n in shape:
            size *= n
        part = small[:, at : at + size].reshape((count,) + shape)
        at += size
        return part

    conv_w_all = taken(LAYERS, taps_count, cw).transpose(1, 2, 0, 3).reshape(LAYERS, taps_count, CONVW)
    conv_b_all = taken(LAYERS, cw).transpose(1, 0, 2).reshape(LAYERS, 1, CONVW)
    gain_in_all = taken(LAYERS, gi).transpose(1, 0, 2).reshape(LAYERS, 1, width)
    gain_out_all = taken(LAYERS, go).transpose(1, 0, 2).reshape(LAYERS, 1, INNER)
    taps_all = jnp.concatenate([conv_w_all, conv_b_all], axis=1)

    layers = []
    for l in range(LAYERS):
        w_rows = jnp.pad(w_in[l, :, INNER:], ((0, 0), (0, ROWS - CONVW - 2 * HEADS)))
        neg_rate = -jnp.exp(head_params[l, 0])
        zero = jnp.zeros((LANES - 2 * HEADS,), f32)
        head = jnp.stack(
            [
                jnp.concatenate([neg_rate, neg_rate, zero]),
                jnp.concatenate([head_params[l, 1], head_params[l, 2], zero]),
            ]
        )
        layers.append(
            dict(
                w_rows=ordered(gathered(w_rows), position),
                w_gate=ordered(gathered(w_in[l, :, :INNER]), position),
                w_out=ordered(gathered(w_out[l]), position),
                taps=taps_all[l],
                gain_in=gain_in_all[l],
                gain_out=gain_out_all[l],
                head=jnp.pad(head, ((0, 6), (0, 0))),
                skip=jnp.repeat(head_params[l, 3], HEAD)[None],
            )
        )
    hidden = tokens.astype(f32)
    stored = []
    for l in range(LAYERS):
        hidden, kept = layer_forward(hidden, layers[l], scalars, hots)
        stored.append(kept)
    result = hidden.astype(bf16)
    grad = cotangent.astype(f32)
    outs = [None] * LAYERS
    heads = [None] * LAYERS
    for l in reversed(range(LAYERS)):
        grad, (gw_rows, gw_gate, gw_out, dtaps, sums_y, sums_h, sums_d) = layer_backward(
            grad, stored[l], layers[l], scalars, hots, owner
        )

        def share(full):
            blocks = full.reshape((count, full.shape[0] // count) + full.shape[1:])
            return summed(jnp.take(blocks, owner, axis=0))

        s_rows, s_gate, s_out = share(gw_rows), share(gw_gate), share(gw_out)
        little = jnp.concatenate(
            [
                dtaps.reshape(8, count, cw).transpose(1, 0, 2).reshape(count, 8 * cw),
                sums_d[0].reshape(count, gi),
                sums_y[0].reshape(count, go),
            ],
            axis=1,
        )
        little_len = little.shape[1]
        little = jnp.pad(little, ((0, 0), (0, -little_len % (8 * LANES)))).reshape(count, -1, LANES)
        little = summed(jnp.take(little, owner, axis=0)).reshape(-1)
        d_taps = little[: 8 * cw].reshape(8, cw)
        outs[l] = (
            little[8 * cw : 8 * cw + gi],
            jnp.concatenate([s_gate, s_rows[:, : CONVW + 2 * HEADS]], axis=1),
            d_taps[:taps_count].T,
            d_taps[taps_count],
            little[8 * cw + gi : 8 * cw + gi + go],
            s_out,
        )
        heads[l] = jnp.stack(
            [
                sums_h[0, :HEADS] + sums_h[0, HEADS : 2 * HEADS],
                sums_h[1, :HEADS],
                sums_h[1, HEADS : 2 * HEADS],
                sums_y[1].reshape(HEADS, HEAD).sum(axis=1),
            ]
        )
    head_total = everywhere(jnp.stack(heads))
    stacked = [jnp.stack([outs[l][member] for l in range(LAYERS)]) for member in range(6)]
    return (result, grad, *stacked, head_total)


def solution(mesh):
    in_specs = (
        P(AXIS, None),
        P(AXIS, None),
        P(),
        P(None, AXIS),
        P(None, AXIS, None),
        P(None, AXIS, None),
        P(None, AXIS),
        P(None, AXIS),
        P(None, AXIS, None),
        P(),
    )
    out_specs = (
        P(AXIS, None),
        P(AXIS, None),
        P(None, AXIS),
        P(None, AXIS, None),
        P(None, AXIS, None),
        P(None, AXIS),
        P(None, AXIS),
        P(None, AXIS, None),
        P(),
    )
    return jax.shard_map(shard_program, mesh=mesh, in_specs=in_specs, out_specs=out_specs, check_vma=False)
```
